128 devices in a mesh: seq: 32 (over x, y, core), head: 4 (over z).
Axes of the slice: x: 4, y: 4, z: 4, core: 2. Of those that a mesh axis runs over, the one named last changes fastest.
Arguments:
- queries: bfloat16 [32768, 2048], P(('seq', 'head')), may hold values from -15 to 15
- key_rows: bfloat16 [32768, 2048], P(('seq', 'head')), may hold values from -15 to 15
- values: bfloat16 [32768, 2048], P(('seq', 'head')), may hold values from -6 to 6
- gate_logits: float32 [16], P('head'), may hold values from -1.5 to 1.5
- out_grad: bfloat16 [32768, 2048], P(('seq', 'head')), may hold values from -6 to 6
Outputs:
- output: bfloat16 [32768, 2048], P(('seq', 'head'))
- query_grad: bfloat16 [32768, 2048], P(('seq', 'head'))
- key_grad: bfloat16 [32768, 2048], P(('seq', 'head'))
- value_grad: bfloat16 [32768, 2048], P(('seq', 'head'))
The draws below stay inside these ranges and needn't reach their ends.
All inputs are finite; a program needn't handle non-finite values.
Results may differ from the reference program's by a relative error of at most 0.0052.
The reference program's roundings to bfloat16 on the way count: a program that leaves them out, or rounds other values in their place, can miss the bound.
Values may be sent and summed in bfloat16 or wider, within the bound.
No kernel may reach another device: no remote copies, remote signals or barrier semaphores. Data moves between devices by JAX's collectives and lax.ppermute only.
A program may use at most 128 MiB of HBM per device.

```python
import jax
import jax.numpy as jnp
from jax import lax

HEADS = 16
DH = 128
SEG = 1024
SEGMENTS = 32
TOKENS = 32768


def drawn_pair(key):
    base = jax.random.fold_in(key, 101)
    key_query, key_keys = jax.random.split(base, 2)
    full_shape = (TOKENS, HEADS * DH)
    query_draw = jnp.clip(jax.random.normal(key_query, full_shape, jnp.float32), -3.0, 3.0)
    key_draw = jnp.clip(jax.random.normal(key_keys, full_shape, jnp.float32), -3.0, 3.0)
    return (query_draw, key_draw)


def shifted(key, salt):
    key_noise, key_offset = jax.random.split(jax.random.fold_in(key, salt))
    full_shape = (SEGMENTS, SEG, HEADS * DH)
    noise = jnp.clip(jax.random.normal(key_noise, full_shape, jnp.float32), -3.0, 3.0)
    offset = jnp.clip(jax.random.normal(key_offset, (SEGMENTS, 1, HEADS * DH), jnp.float32), -3.0, 3.0)
    return (noise + offset).reshape(TOKENS, HEADS * DH)


def draw_queries(key, part):
    return drawn_pair(key)[0].astype(jnp.bfloat16)


def draw_key_rows(key, part):
    return drawn_pair(key)[1].astype(jnp.bfloat16)


def draw_values(key, part):
    return shifted(key, 202).astype(jnp.bfloat16)


def draw_out_grad(key, part):
    return shifted(key, 303).astype(jnp.bfloat16)


def shard_levels(rng, extent, cuts, least, top_value):
    def one(axis_at, blocks):
        heights = jax.random.uniform(jax.random.fold_in(jax.random.fold_in(rng, 6), axis_at), (blocks,), jnp.float32, least / len(cuts), top_value / len(cuts))
        return jnp.repeat(jnp.exp(heights), extent[axis_at] // blocks).reshape((-1,) + (1,) * (len(extent) - axis_at - 1))

    factor_of = one(*cuts[0])
    for cut in cuts[1:]:
        factor_of = factor_of * one(*cut)
    return factor_of


def setup_inputs(seed: int = 0) -> dict:
    splits = jax.random.split(jax.random.key(seed), 6)
    return {
        "queries": draw_queries(jax.random.fold_in(splits[5], 71), 0),
        "key_rows": draw_key_rows(jax.random.fold_in(splits[5], 71), 0),
        "values": draw_values(jax.random.fold_in(splits[5], 71), 0),
        "gate_logits": jnp.clip(jax.random.uniform(splits[3], (HEADS,), jnp.float32, -1.5, 1.5) * shard_levels(splits[3], (HEADS,), ((0, 4),), -0.4, 0.0), -1.5, 1.5),
        "out_grad": draw_out_grad(jax.random.fold_in(splits[5], 71), 0),
    }


highest = lax.Precision.HIGHEST


def feature(inputs):
    return jnp.where(inputs > 0, inputs + 1.0, jnp.exp(jnp.minimum(inputs, 0.0)))


def feature_slope(inputs):
    return jnp.where(inputs > 0, jnp.ones_like(inputs), jnp.exp(jnp.minimum(inputs, 0.0)))


def rounded(inputs):
    return lax.optimization_barrier(inputs.astype(jnp.bfloat16)).astype(jnp.float32)


def memory_part(query_seg, grad_seg, memory, normalizer, gate_share):
    phi_queries = rounded(feature(query_seg.astype(jnp.float32)))
    numerator = jnp.einsum("thd,hde->the", phi_queries, memory, precision=highest)
    raw_denom = jnp.einsum("thd,hd->th", phi_queries, normalizer, precision=highest)
    denominator = jnp.maximum(raw_denom, 1.0)
    retrieved = numerator / denominator[:, :, None]
    grad_wide = grad_seg.astype(jnp.float32)
    numer_grad = gate_share[None, :, None] * grad_wide / denominator[:, :, None]
    denom_grad = jnp.where(raw_denom > 1.0, -gate_share[None, :] * jnp.sum(grad_wide * retrieved, axis=-1) / denominator, 0.0)
    memory_grad = jnp.einsum("thd,the->hde", phi_queries, numer_grad, precision=highest)
    norm_grad = jnp.einsum("th,thd->hd", denom_grad, phi_queries, precision=highest)
    return retrieved, numer_grad, denom_grad, memory_grad, norm_grad


def local_head(inputs):
    query_part, key_part, value_part, grad_part, share = inputs
    score_scale = DH ** -0.5
    scores = jnp.dot(query_part, key_part.T, preferred_element_type=jnp.float32) * score_scale
    causal = jnp.arange(SEG)[:, None] >= jnp.arange(SEG)[None, :]
    scores = jnp.where(causal, scores, -jnp.inf)
    row_max = jnp.max(scores, axis=-1, keepdims=True)
    exp_scores = jnp.exp(scores - row_max)
    weights = exp_scores / jnp.sum(exp_scores, axis=-1, keepdims=True)
    weights_low = weights.astype(jnp.bfloat16)
    local = jnp.dot(weights_low, value_part, preferred_element_type=jnp.float32)
    weight_grad = jnp.dot(grad_part, value_part.T, preferred_element_type=jnp.float32) * (1.0 - share)
    score_grad = weights * (weight_grad - jnp.sum(weights * weight_grad, axis=-1, keepdims=True))
    score_low = score_grad.astype(jnp.bfloat16)
    query_local = jnp.dot(score_low, key_part, preferred_element_type=jnp.float32) * score_scale
    key_local = jnp.dot(score_low.T, query_part, preferred_element_type=jnp.float32) * score_scale
    value_local = jnp.dot(weights_low.T, grad_part, preferred_element_type=jnp.float32) * (1.0 - share)
    return local, query_local, key_local, value_local


def reference(queries, key_rows, values, gate_logits, out_grad):
    full_shape = (SEGMENTS, SEG, HEADS, DH)
    query_all = queries.reshape(full_shape)
    key_all = key_rows.reshape(full_shape)
    value_all = values.reshape(full_shape)
    grad_all = out_grad.reshape(full_shape)
    gate_share = jax.nn.sigmoid(gate_logits.astype(jnp.float32))

    def segment_update(inputs):
        key_seg, value_seg = inputs
        phi_keys = rounded(feature(key_seg.astype(jnp.float32)))
        update = jnp.einsum("thd,the->hde", phi_keys, value_seg.astype(jnp.float32), precision=highest)
        return update, jnp.sum(phi_keys, axis=0)

    updates, key_sums = lax.map(segment_update, (key_all, value_all))
    memory_all = jnp.concatenate([jnp.zeros_like(updates[:1]), jnp.cumsum(updates, axis=0)[:-1]], axis=0)
    normal_all = jnp.concatenate([jnp.zeros_like(key_sums[:1]), jnp.cumsum(key_sums, axis=0)[:-1]], axis=0)

    def segment_grads(inputs):
        query_seg, grad_seg, memory, normalizer = inputs
        parts = memory_part(query_seg, grad_seg, memory, normalizer, gate_share)
        return parts[3], parts[4]

    memory_grads, norm_grads = lax.map(segment_grads, (query_all, grad_all, memory_all, normal_all))
    later_memory = jnp.cumsum(memory_grads[::-1], axis=0)[::-1]
    later_norm = jnp.cumsum(norm_grads[::-1], axis=0)[::-1]
    back_memory_all = jnp.concatenate([later_memory[1:], jnp.zeros_like(later_memory[:1])], axis=0)
    back_norm_all = jnp.concatenate([later_norm[1:], jnp.zeros_like(later_norm[:1])], axis=0)

    def segment_pass(inputs):
        query_seg, key_seg, value_seg, grad_seg, memory, normalizer, back_memory, back_norm = inputs
        retrieved, numer_grad, denom_grad, unused_memory, unused_norm = memory_part(query_seg, grad_seg, memory, normalizer, gate_share)
        local, query_local, key_local, value_local = lax.map(local_head, (query_seg.transpose(1, 0, 2), key_seg.transpose(1, 0, 2), value_seg.transpose(1, 0, 2), grad_seg.transpose(1, 0, 2), gate_share))
        local = local.transpose(1, 0, 2)
        share = gate_share[None, :, None]
        output = (share * retrieved + (1.0 - share) * local).astype(jnp.bfloat16)
        query_wide = query_seg.astype(jnp.float32)
        key_wide = key_seg.astype(jnp.float32)
        value_wide = value_seg.astype(jnp.float32)
        query_grad = query_local.transpose(1, 0, 2) + (jnp.einsum("the,hde->thd", numer_grad, memory, precision=highest) + denom_grad[:, :, None] * normalizer[None]) * feature_slope(query_wide)
        key_grad = key_local.transpose(1, 0, 2) + (jnp.einsum("the,hde->thd", value_wide, back_memory, precision=highest) + back_norm[None]) * feature_slope(key_wide)
        phi_keys = rounded(feature(key_wide))
        value_grad = value_local.transpose(1, 0, 2) + jnp.einsum("thd,hde->the", phi_keys, back_memory, precision=highest)
        return output, query_grad.astype(jnp.bfloat16), key_grad.astype(jnp.bfloat16), value_grad.astype(jnp.bfloat16)

    results = lax.map(segment_pass, (query_all, key_all, value_all, grad_all, memory_all, normal_all, back_memory_all, back_norm_all))
    output, query_grad, key_grad, value_grad = [part.reshape(TOKENS, HEADS * DH) for part in results]
    return (output, query_grad, key_grad, value_grad)
```

```python
import functools

import jax
import jax.numpy as jnp
from jax import lax
from jax.experimental import pallas as pl
from jax.experimental.pallas import tpu as pltpu
from jax.sharding import PartitionSpec as P

DH = 128
HEADS = 4
HALF = 2 * DH
GROUP = HEADS * DH
SHARE = 256
SEG = 4 * SHARE
SCALE = DH ** (-0.5)
LOG2E = 1.4426950408889634
f32 = jnp.float32
bf16 = jnp.bfloat16

ANY = pl.BlockSpec(memory_space=pl.ANY)
VMEM = pl.BlockSpec(memory_space=pltpu.VMEM)
SMEM = pl.BlockSpec(memory_space=pltpu.SMEM)


def shape(dims, dtype=bf16):
    return jax.ShapeDtypeStruct(dims, dtype)


def params(mib=56):
    return pltpu.CompilerParams(vmem_limit_bytes=mib << 20)


def cost(us):
    return pl.CostEstimate(flops=int(us * 5e8), bytes_accessed=int(us * 2e6), transcendentals=0)


def dot(a, b, ca, cb):
    return lax.dot_general(a, b, (((ca,), (cb,)), ((), ())), preferred_element_type=f32)


def feature(x):
    return jnp.where(x > 0, x + 1.0, jnp.exp(jnp.minimum(x, 0.0)))


def slope(x):
    return jnp.where(x > 0, jnp.ones_like(x), jnp.exp(jnp.minimum(x, 0.0)))


def split(x):
    high = x.astype(bf16)
    return high, (x - high.astype(f32)).astype(bf16)


def group_of(z, shift):
    return lax.rem(z + shift + 4, 4)


def run_copies(copies):
    for copy in copies:
        copy.start()
    for copy in copies:
        copy.wait()


def pack_kernel(z_ref, a_ref, b_ref, *rest, parts):
    width = GROUP // parts
    outs, buf, sem_in, sem_out = rest[: 3 * parts], rest[-3], rest[-2], rest[-1]
    z = z_ref[0]
    loads = []
    for shift in (1, 2, 3):
        at = pl.multiple_of(group_of(z, shift) * GROUP, GROUP)
        for i, src in enumerate((a_ref, b_ref)):
            loads.append(
                pltpu.make_async_copy(
                    src.at[:, pl.ds(at, GROUP)], buf.at[shift - 1, i], sem_in.at[shift - 1, i]
                )
            )
    for copy in loads:
        copy.start()
    stores = []
    for shift in (1, 2, 3):
        for i in range(2):
            loads[2 * (shift - 1) + i].wait()
            for part in range(parts):
                copy = pltpu.make_async_copy(
                    buf.at[shift - 1, i, :, pl.ds(part * width, width)],
                    outs[3 * part + shift - 1].at[i],
                    sem_out.at[shift - 1, i, part],
                )
                copy.start()
                stores.append(copy)
    for copy in stores:
        copy.wait()


def pack(z, a, b, parts):
    width = GROUP // parts
    return pl.pallas_call(
        functools.partial(pack_kernel, parts=parts),
        out_shape=[shape((2, SHARE, width))] * (3 * parts),
        in_specs=[SMEM, ANY, ANY],
        out_specs=[ANY] * (3 * parts),
        scratch_shapes=[
            pltpu.VMEM((3, 2, SHARE, GROUP), bf16),
            pltpu.SemaphoreType.DMA((3, 2)),
            pltpu.SemaphoreType.DMA((3, 2, parts)),
        ],
        compiler_params=params(),
        cost_estimate=cost(2),
        name=f"pack{parts}",
    )(z, a, b)


def update_kernel(z_ref, k_ref, v_ref, r1, r2, r3, out_ref, own, sem):
    at = pl.multiple_of(z_ref[0] * GROUP, GROUP)
    run_copies(
        [
            pltpu.make_async_copy(src.at[:, pl.ds(at, GROUP)], own.at[i], sem.at[i])
            for i, src in enumerate((k_ref, v_ref))
        ]
    )
    for head in range(HEADS):
        cols = slice(head * DH, (head + 1) * DH)
        total = jnp.zeros((DH, DH), f32)
        sums = jnp.zeros((1, DH), f32)
        for piece in (own, r1, r2, r3):
            phi = feature(piece[0, :, cols].astype(f32)).astype(bf16)
            total += dot(phi, piece[1, :, cols], 0, 0)
            sums += jnp.sum(phi.astype(f32), axis=0, keepdims=True)
        out_ref[8 * head : 8 * head + 8, :16, :] = total.reshape(8, 16, DH)
        out_ref[8 * head, 16:24, :] = jnp.broadcast_to(sums, (8, DH))


def update(z, keys, values, received):
    return pl.pallas_call(
        update_kernel,
        out_shape=shape((32, 24, DH), f32),
        in_specs=[SMEM, ANY, ANY, VMEM, VMEM, VMEM],
        out_specs=VMEM,
        scratch_shapes=[pltpu.VMEM((2, SHARE, GROUP), bf16), pltpu.SemaphoreType.DMA((2,))],
        compiler_params=params(),
        cost_estimate=cost(2),
        name="update",
    )(z, keys, values, *received)


def scan_kernel(in_ref, out_ref, *, reverse):
    count = in_ref.shape[0]
    total = jnp.zeros(in_ref.shape[1:], f32)
    for step in range(count):
        at = count - 1 - step if reverse else step
        out_ref[at] = total.astype(out_ref.dtype)
        total += in_ref[at].astype(f32)


def scan(x, reverse):
    return pl.pallas_call(
        functools.partial(scan_kernel, reverse=reverse),
        out_shape=shape(x.shape, x.dtype),
        in_specs=[VMEM],
        out_specs=VMEM,
        compiler_params=params(),
        cost_estimate=cost(1),
        name="scan_later" if reverse else "scan_earlier",
    )(x)


def over_segments(x, reverse):
    mine = lax.all_to_all(x, "seq", 0, 0, tiled=True)
    return lax.all_to_all(scan(mine, reverse), "seq", 0, 0, tiled=True)


def attention_kernel(
    z_ref, g_ref, q_ref, k_ref, v_ref, y_ref,
    kv1, kv2, kv3, qy1, qy2, qy3,
    local_ref, dq_ref, o0, o1, o2, o3,
    qs, ks, vs, ys, dks, dvs, dkv, sem_in, sem_out, *, half
):
    z = z_ref[0]
    cols = pl.ds(half * HALF, HALF)
    own = pl.ds(pl.multiple_of(z * GROUP + half * HALF, HALF), HALF)
    copies = []
    for shift in range(4):
        rows = pl.ds(pl.multiple_of(group_of(z, -shift) * SHARE, SHARE), SHARE)
        if shift == 0:
            sources = [r.at[:, own] for r in (q_ref, k_ref, v_ref, y_ref)]
        else:
            kv, qy = (kv1, kv2, kv3)[shift - 1], (qy1, qy2, qy3)[shift - 1]
            sources = [qy.at[0], kv.at[0, :, cols], kv.at[1, :, cols], qy.at[1]]
        for i, (src, dst) in enumerate(zip(sources, (qs, ks, vs, ys))):
            copies.append(pltpu.make_async_copy(src, dst.at[rows], sem_in.at[shift, i]))
    run_copies(copies)

    block = 512

    def one_head(head, carry):
        cs = pl.ds(pl.multiple_of(head * DH, DH), DH)
        rest = 1.0 - g_ref[2 * half + head]
        for i in range(SEG // block):
            rows = slice(i * block, (i + 1) * block)
            last = (i + 1) * block
            old = last - block
            q, y = qs[rows, cs], ys[rows, cs]
            k, v = ks[:last, cs], vs[:last, cs]
            scores = dot(q, k, 1, 1)
            below = lax.broadcasted_iota(jnp.int32, (block, block), 0) >= lax.broadcasted_iota(
                jnp.int32, (block, block), 1
            )
            diagonal = jnp.where(below, scores[:, old:], -jnp.inf)
            scores = jnp.concatenate([scores[:, :old], diagonal], 1) if i else diagonal
            top = jnp.max(scores, 1, keepdims=True)
            powers = jnp.exp2((scores - top) * (SCALE * LOG2E))
            prob = powers * (1.0 / jnp.sum(powers, 1, keepdims=True))
            low = prob.astype(bf16)
            dprob = dot(y, v, 1, 1) * rest
            mean = jnp.sum(prob * dprob, 1, keepdims=True)
            dlow = (prob * (dprob - mean)).astype(bf16)
            local_ref[rows, cs] = dot(low, v, 1, 0)
            dq_ref[rows, cs] = dot(dlow, k, 1, 0) * SCALE
            dv, dk = dot(y, low, 0, 0), dot(q, dlow, 0, 0)
            if i:
                dvs[:, :old] += dv[:, :old]
                dks[:, :old] += dk[:, :old]
            dvs[:, old:last] = dv[:, old:]
            dks[:, old:last] = dk[:, old:]
        dkv[0, :, cs] = (dks[...].T * SCALE).astype(bf16)
        dkv[1, :, cs] = (dvs[...].T * rest).astype(bf16)
        return carry

    lax.fori_loop(0, 2, one_head, 0)
    run_copies(
        [
            pltpu.make_async_copy(
                dkv.at[:, pl.ds(pl.multiple_of(group_of(z, shift) * SHARE, SHARE), SHARE)],
                out,
                sem_out.at[shift],
            )
            for shift, out in enumerate((o0, o1, o2, o3))
        ]
    )


def attention(z, gates, q, k, v, y, kv, qy, half):
    seg_half = (SEG, HALF)
    out = pl.pallas_call(
        functools.partial(attention_kernel, half=half),
        out_shape=[shape(seg_half, f32)] * 2 + [shape((2, SHARE, HALF))] * 4,
        in_specs=[SMEM, SMEM] + [ANY] * 10,
        out_specs=[VMEM, VMEM] + [ANY] * 4,
        scratch_shapes=[pltpu.VMEM(seg_half, bf16)] * 4
        + [pltpu.VMEM((DH, SEG), f32)] * 2
        + [
            pltpu.VMEM((2, SEG, HALF), bf16),
            pltpu.SemaphoreType.DMA((4, 4)),
            pltpu.SemaphoreType.DMA((4,)),
        ],
        compiler_params=params(),
        cost_estimate=cost(10),
        name=f"attention{half}",
    )(z, gates, q, k, v, y, *kv, *qy)
    return out[0], out[1], out[2:]


def memory_kernel(
    z_ref, g_ref, mem_ref, q_ref, y_ref,
    qa1, qa2, qa3, qb1, qb2, qb3, la, lb, da, db,
    mg_ref, o0, o1, o2, o3,
    qs, ys, ls, ds, sem_in, sem_f
):
    z = z_ref[0]
    own = pl.ds(pl.multiple_of(z * GROUP, GROUP), GROUP)
    copies = [
        pltpu.make_async_copy(q_ref.at[:, own], qs.at[0], sem_in.at[0, 0, 0]),
        pltpu.make_async_copy(y_ref.at[:, own], ys.at[0], sem_in.at[0, 0, 1]),
    ]
    for half, pieces in enumerate(((qa1, qa2, qa3), (qb1, qb2, qb3))):
        cols = pl.ds(half * HALF, HALF)
        for shift, piece in enumerate(pieces, 1):
            copies.append(
                pltpu.make_async_copy(piece.at[0], qs.at[shift, :, cols], sem_in.at[half, shift, 0])
            )
            copies.append(
                pltpu.make_async_copy(piece.at[1], ys.at[shift, :, cols], sem_in.at[half, shift, 1])
            )
    for shift in range(4):
        rows = pl.ds(pl.multiple_of(group_of(z, -shift) * SHARE, SHARE), SHARE)
        for half, (lo, dq) in enumerate(((la, da), (lb, db))):
            cols = pl.ds(half * HALF, HALF)
            copies.append(
                pltpu.make_async_copy(lo.at[rows], ls.at[shift, :, cols], sem_f.at[half, shift, 0])
            )
            copies.append(
                pltpu.make_async_copy(dq.at[rows], ds.at[shift, :, cols], sem_f.at[half, shift, 1])
            )
    run_copies(copies)
    outs = (o0, o3, o2, o1)

    def one_head(head, carry):
        cs = pl.ds(pl.multiple_of(head * DH, DH), DH)
        gate = g_ref[head]
        at = pl.multiple_of(head * 8, 8)
        memory = mem_ref[pl.ds(at, 8), :16, :].reshape(DH, DH)
        norm = mem_ref[at, 16:24, :][:1]
        high, low = split(memory)
        right = jnp.concatenate([high, low], 1)
        below = jnp.concatenate([high, low], 0)
        grad = jnp.zeros((DH, 2 * DH), f32)
        norm_grad = jnp.zeros((1, DH), f32)
        for shift in range(4):
            q = qs[shift, :, cs].astype(f32)
            y_low = ys[shift, :, cs]
            y = y_low.astype(f32)
            phi_low = feature(q).astype(bf16)
            phi = phi_low.astype(f32)
            both = dot(phi_low, right, 1, 0)
            raw = jnp.sum(phi * norm, 1, keepdims=True)
            inverse = 1.0 / jnp.maximum(raw, 1.0)
            retrieved = (both[:, :DH] + both[:, DH:]) * inverse
            denom_grad = jnp.where(
                raw > 1.0, -gate * jnp.sum(y * retrieved, 1, keepdims=True) * inverse, 0.0
            )
            weight = gate * inverse
            grad += dot(phi_low, jnp.concatenate(split(y * weight), 1), 0, 0)
            norm_grad += jnp.sum(phi * denom_grad, 0, keepdims=True)
            outs[shift][0, :, cs] = (gate * retrieved + (1.0 - gate) * ls[shift, :, cs]).astype(bf16)
            both = dot(y_low, below, 1, 1)
            back = (both[:, :DH] + both[:, DH:]) * weight + denom_grad * norm
            outs[shift][1, :, cs] = (ds[shift, :, cs] + back * slope(q)).astype(bf16)
        total = grad[:, :DH] + grad[:, DH:]
        mg_ref[pl.ds(at, 8), :16, :] = total.reshape(8, 16, DH).astype(bf16)
        mg_ref[at, 16:32, :] = jnp.broadcast_to(norm_grad, (16, DH)).astype(bf16)
        return carry

    lax.fori_loop(0, HEADS, one_head, 0)


def read_memory(z, gates, memory, q, y, qy_a, qy_b, locals_, dqs):
    out = pl.pallas_call(
        memory_kernel,
        out_shape=[shape((32, 32, DH))] + [shape((2, SHARE, GROUP))] * 4,
        in_specs=[SMEM, SMEM, VMEM] + [ANY] * 12,
        out_specs=[VMEM] * 5,
        scratch_shapes=[pltpu.VMEM((4, SHARE, GROUP), bf16)] * 2
        + [pltpu.VMEM((4, SHARE, GROUP), f32)] * 2
        + [pltpu.SemaphoreType.DMA((2, 4, 2))] * 2,
        compiler_params=params(),
        cost_estimate=cost(5),
        name="read_memory",
    )(z, gates, memory, q, y, *qy_a, *qy_b, *locals_, *dqs)
    return out[0], out[1:]


def gather_kernel(z_ref, p0, p1, p2, p3, a_ref, b_ref):
    for shift, piece in enumerate((p0, p1, p2, p3)):
        cols = pl.ds(pl.multiple_of(group_of(z_ref[0], -shift) * GROUP, GROUP), GROUP)
        a_ref[:, cols] = piece[0]
        b_ref[:, cols] = piece[1]


def gather(z, pieces):
    return pl.pallas_call(
        gather_kernel,
        out_shape=[shape((SHARE, 4 * GROUP))] * 2,
        in_specs=[SMEM] + [VMEM] * 4,
        out_specs=[VMEM] * 2,
        compiler_params=params(),
        cost_estimate=cost(2),
        name="gather",
    )(z, *pieces)


def compact_kernel(in_ref, out_ref):
    out_ref[:GROUP] = in_ref[:, :16, :].reshape(GROUP, DH)
    for head in range(HEADS):
        out_ref[GROUP + 16 * head : GROUP + 16 * head + 16] = in_ref[8 * head, 16:32, :]


def compact(x):
    return pl.pallas_call(
        compact_kernel,
        out_shape=shape((GROUP + 16 * HEADS, DH)),
        in_specs=[VMEM],
        out_specs=VMEM,
        compiler_params=params(),
        cost_estimate=cost(1),
        name="compact",
    )(x)


def key_value_kernel(z_ref, k_ref, v_ref, *rest):
    backs, firsts, seconds = rest[:4], rest[4:8], rest[8:12]
    kg_ref, vg_ref = rest[12:]
    for shift in range(4):
        base = group_of(z_ref[0], -shift) * GROUP
        for head in range(HEADS):
            cols = pl.ds(pl.multiple_of(base + head * DH, DH), DH)
            inner = slice((head % 2) * DH, (head % 2 + 1) * DH)
            grads = (firsts, seconds)[head // 2][shift]
            back = backs[shift][head * DH : (head + 1) * DH]
            norm = backs[shift][GROUP + 16 * head : GROUP + 16 * head + 16].astype(f32)[:1]
            k = k_ref[:, cols].astype(f32)
            v = v_ref[:, cols]
            kg = grads[0, :, inner].astype(f32) + (dot(v, back, 1, 1) + norm) * slope(k)
            kg_ref[:, cols] = kg.astype(bf16)
            vg = grads[1, :, inner].astype(f32) + dot(feature(k).astype(bf16), back, 1, 0)
            vg_ref[:, cols] = vg.astype(bf16)


def key_value(z, keys, values, backs, firsts, seconds):
    return pl.pallas_call(
        key_value_kernel,
        out_shape=[shape((SHARE, 4 * GROUP))] * 2,
        in_specs=[SMEM] + [VMEM] * 14,
        out_specs=[VMEM] * 2,
        compiler_params=params(),
        cost_estimate=cost(4),
        name="key_value",
    )(z, keys, values, *backs, *firsts, *seconds)


def to_peers(blocks):
    return [
        lax.ppermute(block, "head", [(i, (i + shift) % 4) for i in range(4)])
        for shift, block in enumerate(blocks, 1)
    ]


def after(values, *others):
    values = tuple(values)
    return lax.optimization_barrier(values + tuple(others))[: len(values)]


def body(queries, key_rows, values, gate_logits, out_grad):
    z = lax.axis_index("head").astype(jnp.int32).reshape(1)
    gates = jax.nn.sigmoid(gate_logits)
    kv = to_peers(pack(z, key_rows, values, 1))
    blocks = pack(z, queries, out_grad, 2)
    qy_a = to_peers(after(blocks[:3], *kv))
    qy_b = to_peers(after(blocks[3:], *qy_a))
    memory = over_segments(update(z, key_rows, values, kv), False)
    local_a, dq_a, dkv_a = attention(z, gates, queries, key_rows, values, out_grad, kv, qy_a, 0)
    back_a = to_peers(dkv_a[1:])
    local_b, dq_b, dkv_b = attention(z, gates, queries, key_rows, values, out_grad, kv, qy_b, 1)
    back_b = to_peers(dkv_b[1:])
    grads, oq = read_memory(
        z, gates, memory, queries, out_grad, qy_a, qy_b, (local_a, local_b), (dq_a, dq_b)
    )
    oq_back = to_peers(oq[1:])
    state = compact(over_segments(grads, True))
    states = [state] + to_peers([state] * 3)
    output, query_grad = gather(z, [oq[0], *oq_back])
    key_grad, value_grad = key_value(
        z, key_rows, values, states, [dkv_a[0], *back_a], [dkv_b[0], *back_b]
    )
    return output, query_grad, key_grad, value_grad


def solution(mesh):
    spec = P(("seq", "head"), None)
    return jax.shard_map(
        body,
        mesh=mesh,
        in_specs=(spec, spec, spec, P("head"), spec),
        out_specs=(spec,) * 4,
        check_vma=False,
    )
```

```python
import functools

import jax
import jax.numpy as jnp
from jax import lax
from jax.experimental import pallas as pl
from jax.experimental.pallas import tpu as pltpu
from jax.sharding import PartitionSpec as P


DH = 128
HEADS = 4
HALF = 2 * DH
GROUP = HEADS * DH
ROWS = GROUP + 16 * HEADS
SHARE = 256
SEG = 4 * SHARE
SCALE = DH ** (-0.5)
LOG2E = 1.4426950408889634
f32 = jnp.float32
bf16 = jnp.bfloat16

HBM = pl.BlockSpec(memory_space=pltpu.HBM)
VMEM = pl.BlockSpec(memory_space=pltpu.VMEM)
SMEM = pl.BlockSpec(memory_space=pltpu.SMEM)


def shape(dims, dtype=bf16):
    return jax.ShapeDtypeStruct(dims, dtype)


def params(mib=56):
    return pltpu.CompilerParams(vmem_limit_bytes=mib << 20)


def cost(us):
    return pl.CostEstimate(flops=int(us * 5e8), bytes_accessed=int(us * 2e6), transcendentals=0)


def dot(a, b, ca, cb):
    return lax.dot_general(a, b, (((ca,), (cb,)), ((), ())), preferred_element_type=f32)


def feature(x):
    return jnp.where(x > 0, x + 1.0, jnp.exp(jnp.minimum(x, 0.0)))


def slope(x):
    return jnp.where(x > 0, jnp.ones_like(x), jnp.exp(jnp.minimum(x, 0.0)))


def split(x):
    high = x.astype(bf16)
    return high, (x - high.astype(f32)).astype(bf16)


def group_of(z, shift):
    return lax.rem(z + shift + 4, 4)


def run_copies(copies):
    for copy in copies:
        copy.start()
    for copy in copies:
        copy.wait()


def front_kernel(z_ref, k_ref, v_ref, q_ref, y_ref, *rest):
    partials, own_ref, firsts, seconds = rest[:3], rest[3], rest[4:7], rest[7:10]
    buf, sem_in, sem_out = rest[10:]
    z = z_ref[0]
    loads, stores = [], []
    for shift in (1, 2, 3):
        at = pl.multiple_of(group_of(z, shift) * GROUP, GROUP)
        for i, src in enumerate((k_ref, v_ref, q_ref, y_ref)):
            here = (shift - 1, i)
            for half, outs in enumerate((firsts, seconds)):
                cols = pl.ds(half * HALF, HALF)
                stores.append(
                    pltpu.make_async_copy(
                        buf.at[shift - 1, i, :, cols],
                        outs[shift - 1].at[i],
                        sem_out.at[shift - 1, i, half],
                    )
                )
            if i >= 2:
                copy = pltpu.make_async_copy(
                    src.at[:, pl.ds(at, GROUP)], buf.at[here], sem_in.at[shift - 1, i - 2]
                )
                copy.start()
                loads.append(copy)
            else:
                buf[here] = src[:, pl.ds(at, GROUP)]
                stores[-1].start()
                stores[-2].start()
    for shift in (1, 2, 3, 0):
        base = group_of(z, shift) * GROUP
        out = own_ref if shift == 0 else partials[shift - 1]
        for head in range(HEADS):
            cols = pl.ds(pl.multiple_of(base + head * DH, DH), DH)
            phi = feature(k_ref[:, cols].astype(f32)).astype(bf16)
            out[head * DH : (head + 1) * DH] = dot(phi, v_ref[:, cols], 0, 0).astype(out.dtype)
            sums = jnp.sum(phi.astype(f32), axis=0, keepdims=True)
            high = sums.astype(bf16).astype(f32)
            first = lax.broadcasted_iota(jnp.int32, (16, DH), 0) == 0
            rows = jnp.where(first, jnp.broadcast_to(high, (16, DH)), sums - high)
            out[GROUP + 16 * head : GROUP + 16 * head + 16] = rows.astype(out.dtype)
    for j, copy in enumerate(loads):
        copy.wait()
        at = 8 * (j // 2) + 2 * (2 + j % 2)
        stores[at].start()
        stores[at + 1].start()
    for copy in stores:
        copy.wait()


def front(z, k, v, q, y):
    out = pl.pallas_call(
        front_kernel,
        out_shape=[shape((ROWS, DH))] * 3
        + [shape((ROWS, DH), f32)]
        + [shape((4, SHARE, HALF))] * 6,
        in_specs=[SMEM, VMEM, VMEM, HBM, HBM],
        out_specs=[VMEM] * 4 + [HBM] * 6,
        scratch_shapes=[
            pltpu.VMEM((3, 4, SHARE, GROUP), bf16),
            pltpu.SemaphoreType.DMA((3, 2)),
            pltpu.SemaphoreType.DMA((3, 4, 2)),
        ],
        compiler_params=params(),
        cost_estimate=cost(6),
        name="front",
    )(z, k, v, q, y)
    return out[:3], out[3], out[4:7], out[7:10]


def update_kernel(own, r1, r2, r3, out_ref):
    for head in range(HEADS):
        rows = slice(head * DH, (head + 1) * DH)
        total = own[rows]
        for piece in (r1, r2, r3):
            total += piece[rows].astype(f32)
        out_ref[8 * head : 8 * head + 8, :16, :] = total.reshape(8, 16, DH)
        rows = slice(GROUP + 16 * head, GROUP + 16 * head + 16)
        sums = own[rows]
        for piece in (r1, r2, r3):
            sums += piece[rows].astype(f32)
        out_ref[8 * head, 16:24, :] = jnp.broadcast_to(sums[:1] + sums[1:2], (8, DH))


def update(own, received):
    return pl.pallas_call(
        update_kernel,
        out_shape=shape((32, 24, DH), f32),
        in_specs=[VMEM] * 4,
        out_specs=VMEM,
        compiler_params=params(),
        cost_estimate=cost(2),
        name="update",
    )(own, *received)


def scan_kernel(in_ref, out_ref, *, reverse):
    count = in_ref.shape[0]
    total = jnp.zeros(in_ref.shape[1:], f32)
    for step in range(count):
        at = count - 1 - step if reverse else step
        out_ref[at] = total.astype(out_ref.dtype)
        total += in_ref[at].astype(f32)


def scan(x, reverse):
    return pl.pallas_call(
        functools.partial(scan_kernel, reverse=reverse),
        out_shape=shape(x.shape, x.dtype),
        in_specs=[VMEM],
        out_specs=VMEM,
        compiler_params=params(),
        cost_estimate=cost(2),
        name="scan_later" if reverse else "scan_earlier",
    )(x)


def memory_of(mem_ref, head):
    at = pl.multiple_of(head * 8, 8)
    memory = mem_ref[pl.ds(at, 8), :16, :].reshape(DH, DH)
    high, low = split(memory)
    norm = mem_ref[at, 16:24, :][:1]
    return jnp.concatenate([high, low], 1), jnp.concatenate([high, low], 0), norm


def read_rows(memory, gate, q, y_low):
    right, _, norm = memory
    y = y_low.astype(f32)
    phi_low = feature(q).astype(bf16)
    phi = phi_low.astype(f32)
    both = dot(phi_low, right, 1, 0)
    raw = jnp.sum(phi * norm, 1, keepdims=True)
    inverse = 1.0 / jnp.maximum(raw, 1.0)
    retrieved = (both[:, :DH] + both[:, DH:]) * inverse
    denom_grad = jnp.where(
        raw > 1.0, -gate * jnp.sum(y * retrieved, 1, keepdims=True) * inverse, 0.0
    )
    return phi_low, phi, retrieved, denom_grad, gate * inverse


def results_of_rows(memory, gate, q, y_low, retrieved, denom_grad, weight, local, dq):
    _, below, norm = memory
    both = dot(y_low, below, 1, 1)
    back = (both[:, :DH] + both[:, DH:]) * weight + denom_grad * norm
    out = gate * retrieved + (1.0 - gate) * local
    return out.astype(bf16), (dq + back * slope(q)).astype(bf16)


def attention_kernel(
    z_ref, g_ref, k_ref, v_ref, q_ref, y_ref, r1, r2, r3, *refs, half
):
    refs = list(refs)
    mem_ref = refs.pop(0) if half else None
    if half:
        outs = [refs.pop(0) for _ in range(4)]
        local_ref, dq_ref, dkv_ref, sem_out = [refs.pop() for _ in range(4)]
    else:
        local_ref, dq_ref, dkv_ref = [refs.pop(0) for _ in range(3)]
    ks, vs, qs, ys, dks, dvs, sem = refs
    z = z_ref[0]
    own = pl.ds(pl.multiple_of(z * GROUP + half * HALF, HALF), HALF)
    copies = []
    for shift in range(4):
        rows = pl.ds(pl.multiple_of(group_of(z, -shift) * SHARE, SHARE), SHARE)
        for i, (src, dst) in enumerate(zip((k_ref, v_ref, q_ref, y_ref), (ks, vs, qs, ys))):
            block = src.at[:, own] if shift == 0 else (r1, r2, r3)[shift - 1].at[i]
            copies.append(pltpu.make_async_copy(block, dst.at[rows], sem.at[shift, i]))
    run_copies(copies)

    block = 512

    def one_head(head, carry):
        cs = pl.ds(pl.multiple_of(head * DH, DH), DH)
        rest = 1.0 - g_ref[2 * half + head]
        for i in range(SEG // block):
            rows = slice(i * block, (i + 1) * block)
            last = (i + 1) * block
            old = last - block
            q, y = qs[rows, cs], ys[rows, cs]
            k, v = ks[:last, cs], vs[:last, cs]
            scores = dot(q, k, 1, 1)
            below = lax.broadcasted_iota(jnp.int32, (block, block), 0) >= lax.broadcasted_iota(
                jnp.int32, (block, block), 1
            )
            diagonal = jnp.where(below, scores[:, old:], -jnp.inf)
            scores = jnp.concatenate([scores[:, :old], diagonal], 1) if i else diagonal
            top = jnp.max(scores, 1, keepdims=True)
            powers = jnp.exp2((scores - top) * (SCALE * LOG2E))
            prob = powers * (1.0 / jnp.sum(powers, 1, keepdims=True))
            low = prob.astype(bf16)
            dprob = dot(y, v, 1, 1) * rest
            mean = jnp.sum(prob * dprob, 1, keepdims=True)
            dlow = (prob * (dprob - mean)).astype(bf16)
            local_ref[rows, cs] = dot(low, v, 1, 0)
            dq_ref[rows, cs] = dot(dlow, k, 1, 0) * SCALE
            dv, dk = dot(y, low, 0, 0), dot(q, dlow, 0, 0)
            if i:
                dvs[:, :old] += dv[:, :old]
                dks[:, :old] += dk[:, :old]
            dvs[:, old:last] = dv[:, old:]
            dks[:, old:last] = dk[:, old:]
        dkv_ref[0, :, cs] = (dks[...].T * SCALE).astype(bf16)
        dkv_ref[1, :, cs] = (dvs[...].T * rest).astype(bf16)
        if half:
            gate = g_ref[2 * half + head]
            memory = memory_of(mem_ref, 2 * half + head)
            for i in range(4):
                rows = slice(i * SHARE, (i + 1) * SHARE)
                q, y = qs[rows, cs].astype(f32), ys[rows, cs]
                _, _, retrieved, denom_grad, weight = read_rows(memory, gate, q, y)
                out, dq = results_of_rows(
                    memory, gate, q, y, retrieved, denom_grad, weight,
                    local_ref[rows, cs], dq_ref[rows, cs],
                )
                dkv_ref[2, rows, cs] = out
                dkv_ref[3, rows, cs] = dq
        return carry

    lax.fori_loop(0, 2, one_head, 0)
    if half:
        run_copies(
            [
                pltpu.make_async_copy(
                    dkv_ref.at[:, pl.ds(pl.multiple_of(group_of(z, i) * SHARE, SHARE), SHARE)],
                    out,
                    sem_out.at[i],
                )
                for i, out in enumerate(outs)
            ]
        )


def attention(z, gates, arrays, received, half, memory=()):
    seg_half = (SEG, HALF)
    last = [
        pltpu.SemaphoreType.DMA((4,)),
        pltpu.VMEM((4, SEG, HALF), bf16),
        pltpu.VMEM(seg_half, f32),
        pltpu.VMEM(seg_half, f32),
    ]
    return pl.pallas_call(
        functools.partial(attention_kernel, half=half),
        out_shape=[shape((4, SHARE, HALF))] * 4
        if half
        else [shape(seg_half, f32)] * 2 + [shape((2, SEG, HALF))],
        in_specs=[SMEM, SMEM] + [HBM] * 7 + [VMEM] * half,
        out_specs=[HBM] * 4 if half else [VMEM] * 3,
        scratch_shapes=[pltpu.VMEM(seg_half, bf16)] * 4
        + [pltpu.VMEM((DH, SEG), f32)] * 2
        + [pltpu.SemaphoreType.DMA((4, 4))]
        + last * half,
        compiler_params=params(),
        cost_estimate=cost(12 if half else 10),
    )(z, gates, *arrays, *received, *memory)


def memory_kernel(*refs, half, grads, results):
    z_ref, g_ref, mem_ref, q_ref, y_ref, r1, r2, r3 = refs[:8]
    refs = list(refs[8:])
    local_ref, dq_ref, dkv_ref = [refs.pop(0) for _ in range(3)] if results else [None] * 3
    earlier = refs.pop(0) if grads and half else None
    mg_ref = refs.pop(0) if grads else None
    outs = [refs.pop(0) for _ in range(4)] if results else None
    qs, ys, sem = refs[:3]
    ls, ds, kvs, sem_f = refs[3:] if results else [None] * 4
    z = z_ref[0]
    own = pl.ds(pl.multiple_of(z * GROUP + half * HALF, HALF), HALF)
    copies = []
    for shift in range(4):
        for i, (src, dst) in enumerate(((q_ref, qs), (y_ref, ys))):
            block = src.at[:, own] if shift == 0 else (r1, r2, r3)[shift - 1].at[2 + i]
            copies.append(pltpu.make_async_copy(block, dst.at[shift], sem.at[shift, i]))
        if results:
            rows = pl.ds(pl.multiple_of(group_of(z, -shift) * SHARE, SHARE), SHARE)
            for i, (src, dst) in enumerate(
                ((local_ref.at[rows], ls), (dq_ref.at[rows], ds), (dkv_ref.at[:, rows], kvs))
            ):
                copies.append(pltpu.make_async_copy(src, dst.at[shift], sem_f.at[shift, i]))
    run_copies(copies)
    if results:
        outs = [outs[(4 - shift) % 4] for shift in range(4)]
        for shift in range(4):
            outs[shift][:2] = kvs[shift]
    if earlier is not None:
        mg_ref[:16] = earlier[...]
    start = 16 if earlier is not None else 0

    def one_head(head, carry):
        cs = pl.ds(pl.multiple_of(head * DH, DH), DH)
        gate = g_ref[2 * half + head]
        memory = memory_of(mem_ref, 2 * half + head)
        grad = jnp.zeros((DH, 2 * DH), f32)
        norm_grad = jnp.zeros((1, DH), f32)
        for shift in range(4):
            q, y = qs[shift, :, cs].astype(f32), ys[shift, :, cs]
            phi_low, phi, retrieved, denom_grad, weight = read_rows(memory, gate, q, y)
            if grads:
                scaled = split(y.astype(f32) * weight)
                grad += dot(phi_low, jnp.concatenate(scaled, 1), 0, 0)
                norm_grad += jnp.sum(phi * denom_grad, 0, keepdims=True)
            if results:
                out, dq = results_of_rows(
                    memory, gate, q, y, retrieved, denom_grad, weight,
                    ls[shift, :, cs], ds[shift, :, cs],
                )
                outs[shift][2, :, cs] = out
                outs[shift][3, :, cs] = dq
        if grads:
            total = grad[:, :DH] + grad[:, DH:]
            at = pl.multiple_of(start + head * 8, 8)
            mg_ref[pl.ds(at, 8), :16, :] = total.reshape(8, 16, DH).astype(bf16)
            mg_ref[at, 16:32, :] = jnp.broadcast_to(norm_grad, (16, DH)).astype(bf16)
        return carry

    lax.fori_loop(0, 2, one_head, 0)


def read_memory(z, gates, memory, q, y, received, half, earlier=None, local=None, grads=True):
    results = local is not None
    join = grads and half
    out = pl.pallas_call(
        functools.partial(memory_kernel, half=half, grads=grads, results=results),
        out_shape=[shape((32 if half else 16, 32, DH))] * grads
        + [shape((4, SHARE, HALF))] * (4 * results),
        in_specs=[SMEM, SMEM, VMEM] + [HBM] * 5 + [HBM] * (3 * results) + [VMEM] * bool(join),
        out_specs=[VMEM] * (grads + 4 * results),
        scratch_shapes=[pltpu.VMEM((4, SHARE, HALF), bf16)] * 2
        + [pltpu.SemaphoreType.DMA((4, 2))]
        + (
            [pltpu.VMEM((4, SHARE, HALF), f32)] * 2
            + [pltpu.VMEM((4, 2, SHARE, HALF), bf16), pltpu.SemaphoreType.DMA((4, 3))]
        )
        * results,
        compiler_params=params(),
        cost_estimate=cost(4),
    )(z, gates, memory, q, y, *received, *(local or ()), *([earlier] if join else []))
    return (out[0], out[1:]) if grads else out


def token_kernel(z_ref, *rest):
    firsts, seconds, (a_ref, b_ref) = rest[:4], rest[4:8], rest[8:]
    for shift in range(4):
        base = group_of(z_ref[0], -shift) * GROUP
        for half, pieces in enumerate((firsts, seconds)):
            cols = pl.ds(pl.multiple_of(base + half * HALF, HALF), HALF)
            a_ref[:, cols] = pieces[shift][0]
            b_ref[:, cols] = pieces[shift][1]


def results_of_tokens(z, firsts, seconds):
    piece = pl.BlockSpec((2, SHARE, HALF), lambda i: (1, 0, 0))
    whole = pl.BlockSpec((SHARE, 4 * GROUP), lambda i: (0, 0))
    return pl.pallas_call(
        token_kernel,
        grid=(1,),
        out_shape=[shape((SHARE, 4 * GROUP))] * 2,
        in_specs=[SMEM] + [piece] * 8,
        out_specs=[whole] * 2,
        compiler_params=params(),
        cost_estimate=cost(3),
        name="results",
    )(z, *firsts, *seconds)


def compact_kernel(in_ref, out_ref):
    out_ref[:GROUP] = in_ref[:, :16, :].reshape(GROUP, DH)
    for head in range(HEADS):
        out_ref[GROUP + 16 * head : GROUP + 16 * head + 16] = in_ref[8 * head, 16:32, :]


def compact(x):
    return pl.pallas_call(
        compact_kernel,
        out_shape=shape((ROWS, DH)),
        in_specs=[VMEM],
        out_specs=VMEM,
        compiler_params=params(),
        cost_estimate=cost(2),
        name="compact",
    )(x)


def key_value_kernel(z_ref, k_ref, v_ref, *rest):
    backs, firsts, seconds = rest[:4], rest[4:8], rest[8:12]
    kg_ref, vg_ref = rest[12:]
    for shift in range(4):
        base = group_of(z_ref[0], -shift) * GROUP
        for head in range(HEADS):
            cols = pl.ds(pl.multiple_of(base + head * DH, DH), DH)
            inner = slice((head % 2) * DH, (head % 2 + 1) * DH)
            grads = (firsts, seconds)[head // 2][shift]
            back = backs[shift][head * DH : (head + 1) * DH]
            norm = backs[shift][GROUP + 16 * head : GROUP + 16 * head + 16].astype(f32)[:1]
            k = k_ref[:, cols].astype(f32)
            v = v_ref[:, cols]
            kg = grads[0, :, inner].astype(f32) + (dot(v, back, 1, 1) + norm) * slope(k)
            kg_ref[:, cols] = kg.astype(bf16)
            vg = grads[1, :, inner].astype(f32) + dot(feature(k).astype(bf16), back, 1, 0)
            vg_ref[:, cols] = vg.astype(bf16)


def key_value(z, keys, values, backs, firsts, seconds):
    piece = pl.BlockSpec((2, SHARE, HALF), lambda i: (0, 0, 0))
    whole = pl.BlockSpec((SHARE, 4 * GROUP), lambda i: (0, 0))
    state = pl.BlockSpec((ROWS, DH), lambda i: (0, 0))
    return pl.pallas_call(
        key_value_kernel,
        grid=(1,),
        out_shape=[shape((SHARE, 4 * GROUP))] * 2,
        in_specs=[SMEM] + [whole] * 2 + [state] * 4 + [piece] * 8,
        out_specs=[whole] * 2,
        compiler_params=params(),
        cost_estimate=cost(5),
        name="key_value",
    )(z, keys, values, *backs, *firsts, *seconds)


def to_peers(blocks):
    sent = []
    for shift, block in enumerate(blocks, 1):
        sent.append(lax.ppermute(block, "head", [(i, (i + shift) % 4) for i in range(4)]))
    return sent


def swap(x):
    return lax.all_to_all(x, "seq", 0, 0, tiled=True)


def body(k, v, q, y, gate_logits):
    z = lax.axis_index("head").astype(jnp.int32).reshape(1)
    gates = jax.nn.sigmoid(gate_logits)
    arrays = (k, v, q, y)
    partials, own, firsts, seconds = front(z, *arrays)
    partials = to_peers(partials)
    in_a = to_peers(firsts)
    in_b = to_peers(seconds)
    slices = swap(update(own, partials))
    memory = swap(scan(slices, False))
    local_a = attention(z, gates, arrays, in_a, 0)
    grads, out_a = read_memory(z, gates, memory, q, y, in_a, 0, local=local_a)
    back_a = to_peers(out_a[1:])
    grads, _ = read_memory(z, gates, memory, q, y, in_b, 1, earlier=grads)
    slices = swap(grads)
    out_b = attention(z, gates, arrays, in_b, 1, [memory])
    back_b = to_peers(out_b[1:])
    state = compact(swap(scan(slices, True)))
    states = [state] + to_peers([state] * 3)
    firsts, seconds = [out_a[0], *back_a], [out_b[0], *back_b]
    output, query_grad = results_of_tokens(z, firsts, seconds)
    key_grad, value_grad = key_value(z, k, v, states, firsts, seconds)
    return output, query_grad, key_grad, value_grad


def whole(queries, key_rows, values, gate_logits, out_grad):
    return body(key_rows, values, queries, out_grad, gate_logits)


def solution(mesh):
    spec = P(("seq", "head"), None)
    return jax.shard_map(
        whole,
        mesh=mesh,
        in_specs=(spec, spec, spec, P("head"), spec),
        out_specs=(spec,) * 4,
        check_vma=False,
    )
```

```python
import functools

import jax
import jax.numpy as jnp
from jax import lax
from jax.experimental import pallas as pl
from jax.experimental.pallas import tpu as pltpu
from jax.sharding import PartitionSpec as P


DH = 128
HEADS = 4
HALF = 2 * DH
GROUP = HEADS * DH
ROWS = GROUP + 16 * HEADS
SHARE = 256
SEG = 4 * SHARE
SCALE = DH ** (-0.5)
LOG2E = 1.4426950408889634
f32 = jnp.float32
bf16 = jnp.bfloat16

HBM = pl.BlockSpec(memory_space=pltpu.HBM)
VMEM = pl.BlockSpec(memory_space=pltpu.VMEM)
SMEM = pl.BlockSpec(memory_space=pltpu.SMEM)


def shape(dims, dtype=bf16):
    return jax.ShapeDtypeStruct(dims, dtype)


def params(mib=56):
    return pltpu.CompilerParams(vmem_limit_bytes=mib << 20)


def cost(us):
    return pl.CostEstimate(flops=int(us * 5e8), bytes_accessed=int(us * 2e6), transcendentals=0)


def dot(a, b, ca, cb):
    return lax.dot_general(a, b, (((ca,), (cb,)), ((), ())), preferred_element_type=f32)


def feature(x):
    return jnp.where(x > 0, x + 1.0, jnp.exp(jnp.minimum(x, 0.0)))


def slope(x):
    return jnp.where(x > 0, jnp.ones_like(x), jnp.exp(jnp.minimum(x, 0.0)))


def split(x):
    high = x.astype(bf16)
    return high, (x - high.astype(f32)).astype(bf16)


def group_of(z, shift):
    return lax.rem(z + shift + 4, 4)


def run_copies(copies):
    for copy in copies:
        copy.start()
    for copy in copies:
        copy.wait()


def front_kernel(z_ref, k_ref, v_ref, q_ref, y_ref, *rest):
    partials, own_ref, outs = rest[:3], rest[3], (rest[4:7], rest[7:10], rest[10:13])
    buf, sem_in, sem_out = rest[13:]
    z = z_ref[0]
    loads, late, stores = [], [], []
    for shift in (1, 2, 3):
        at = pl.multiple_of(group_of(z, shift) * GROUP, GROUP)
        first, queries, keys = [group[shift - 1] for group in outs]
        for i, src in enumerate((k_ref, v_ref)):
            sem = sem_out.at[shift - 1, i]
            cols = pl.ds(at, HALF)
            stores.append(pltpu.make_async_copy(src.at[:, cols], first.at[i], sem.at[0]))
            cols = pl.ds(pl.multiple_of(at + HALF, HALF), HALF)
            stores.append(pltpu.make_async_copy(src.at[:, cols], keys.at[i], sem.at[1]))
        for i, src in enumerate((q_ref, y_ref)):
            part, sem = buf.at[shift - 1, i], sem_out.at[shift - 1, 2 + i]
            cols = pl.ds(at, GROUP)
            loads.append(pltpu.make_async_copy(src.at[:, cols], part, sem_in.at[shift - 1, i]))
            late.append(
                (
                    pltpu.make_async_copy(part.at[:, pl.ds(0, HALF)], first.at[2 + i], sem.at[0]),
                    pltpu.make_async_copy(part.at[:, pl.ds(HALF, HALF)], queries.at[i], sem.at[1]),
                )
            )
    for copy in loads + stores:
        copy.start()
    for step, shift in enumerate((1, 2, 3, 0)):
        base = group_of(z, shift) * GROUP
        out = own_ref if shift == 0 else partials[shift - 1]
        for head in range(HEADS):
            cols = pl.ds(pl.multiple_of(base + head * DH, DH), DH)
            phi = feature(k_ref[:, cols].astype(f32)).astype(bf16)
            out[head * DH : (head + 1) * DH] = dot(phi, v_ref[:, cols], 0, 0).astype(out.dtype)
            sums = jnp.sum(phi.astype(f32), axis=0, keepdims=True)
            high = sums.astype(bf16).astype(f32)
            first = lax.broadcasted_iota(jnp.int32, (16, DH), 0) == 0
            rows = jnp.where(first, jnp.broadcast_to(high, (16, DH)), sums - high)
            out[GROUP + 16 * head : GROUP + 16 * head + 16] = rows.astype(out.dtype)
        if step == 1:
            for copy, pair in zip(loads, late):
                copy.wait()
                for store in pair:
                    store.start()
                    stores.append(store)
    for copy in stores:
        copy.wait()


def front(z, k, v, q, y):
    out = pl.pallas_call(
        front_kernel,
        out_shape=[shape((ROWS, DH))] * 3
        + [shape((ROWS, DH), f32)]
        + [shape((4, SHARE, HALF))] * 3
        + [shape((2, SHARE, HALF))] * 6,
        in_specs=[SMEM, VMEM, VMEM, HBM, HBM],
        out_specs=[VMEM] * 4 + [HBM] * 9,
        scratch_shapes=[
            pltpu.VMEM((3, 2, SHARE, GROUP), bf16),
            pltpu.SemaphoreType.DMA((3, 2)),
            pltpu.SemaphoreType.DMA((3, 4, 2)),
        ],
        compiler_params=params(60),
        cost_estimate=cost(6),
        name="front",
    )(z, k, v, q, y)
    return out[:3], out[3], out[4:7], out[7:10], out[10:13]


def update_kernel(own, r1, r2, r3, out_ref):
    for head in range(HEADS):
        rows = slice(head * DH, (head + 1) * DH)
        total = own[rows]
        for piece in (r1, r2, r3):
            total += piece[rows].astype(f32)
        out_ref[8 * head : 8 * head + 8, :16, :] = total.reshape(8, 16, DH)
        rows = slice(GROUP + 16 * head, GROUP + 16 * head + 16)
        sums = own[rows]
        for piece in (r1, r2, r3):
            sums += piece[rows].astype(f32)
        out_ref[8 * head, 16:24, :] = jnp.broadcast_to(sums[:1] + sums[1:2], (8, DH))


def update(own, received):
    return pl.pallas_call(
        update_kernel,
        out_shape=shape((32, 24, DH), f32),
        in_specs=[VMEM] * 4,
        out_specs=VMEM,
        compiler_params=params(8),
        cost_estimate=cost(2),
        name="update",
    )(own, *received)


def scan_kernel(in_ref, out_ref, buf, res, sem_in, sem_out, *, reverse):
    count, parts = in_ref.shape[0], 4
    each = count // parts
    order = list(range(parts))[::-1] if reverse else list(range(parts))
    loads, stores = [], []
    for part in range(parts):
        at = pl.ds(part * each, each)
        loads.append(pltpu.make_async_copy(in_ref.at[at], buf.at[at], sem_in.at[part]))
        stores.append(pltpu.make_async_copy(res.at[at], out_ref.at[at], sem_out.at[part]))
    for part in order:
        loads[part].start()
    total = jnp.zeros(in_ref.shape[1:], f32)
    for part in order:
        loads[part].wait()
        for step in range(each):
            at = part * each + (each - 1 - step if reverse else step)
            res[at] = total.astype(res.dtype)
            total += buf[at].astype(f32)
        stores[part].start()
    for copy in stores:
        copy.wait()


def scan(x, reverse):
    return pl.pallas_call(
        functools.partial(scan_kernel, reverse=reverse),
        out_shape=shape(x.shape, x.dtype),
        in_specs=[HBM],
        out_specs=HBM,
        scratch_shapes=[pltpu.VMEM(x.shape, x.dtype)] * 2 + [pltpu.SemaphoreType.DMA((4,))] * 2,
        compiler_params=params(12),
        cost_estimate=cost(2),
        name="scan_later" if reverse else "scan_earlier",
    )(x)


def memory_of(mem_ref, head):
    at = pl.multiple_of(head * 8, 8)
    memory = mem_ref[pl.ds(at, 8), :16, :].reshape(DH, DH)
    high, low = split(memory)
    norm = mem_ref[at, 16:24, :][:1]
    return jnp.concatenate([high, low], 1), jnp.concatenate([high, low], 0), norm


def read_rows(memory, gate, q, y_low):
    right, _, norm = memory
    y = y_low.astype(f32)
    phi_low = feature(q).astype(bf16)
    phi = phi_low.astype(f32)
    both = dot(phi_low, right, 1, 0)
    raw = jnp.sum(phi * norm, 1, keepdims=True)
    inverse = 1.0 / jnp.maximum(raw, 1.0)
    retrieved = (both[:, :DH] + both[:, DH:]) * inverse
    denom_grad = jnp.where(
        raw > 1.0, -gate * jnp.sum(y * retrieved, 1, keepdims=True) * inverse, 0.0
    )
    return phi_low, phi, retrieved, denom_grad, gate * inverse


def results_of_rows(memory, gate, q, y_low, retrieved, denom_grad, weight, local, dq):
    _, below, norm = memory
    both = dot(y_low, below, 1, 1)
    back = (both[:, :DH] + both[:, DH:]) * weight + denom_grad * norm
    out = gate * retrieved + (1.0 - gate) * local
    return out.astype(bf16), (dq + back * slope(q)).astype(bf16)


def attention_kernel(
    z_ref, g_ref, k_ref, v_ref, q_ref, y_ref, *refs, half
):
    refs = list(refs)
    received = [[refs.pop(0) for _ in range(3)] for _ in range(1 + half)]
    mem_ref = refs.pop(0) if half else None
    if half:
        outs = [refs.pop(0) for _ in range(4)]
        local_ref, dq_ref, dkv_ref, sem_out = [refs.pop() for _ in range(4)]
    else:
        local_ref, dq_ref, dkv_ref = [refs.pop(0) for _ in range(3)]
    ks, vs, qs, ys, dks, dvs, sem = refs
    z = z_ref[0]
    own = pl.ds(pl.multiple_of(z * GROUP + half * HALF, HALF), HALF)
    copies = []
    for shift in range(4):
        rows = pl.ds(pl.multiple_of(group_of(z, -shift) * SHARE, SHARE), SHARE)
        for i, (src, dst) in enumerate(zip((k_ref, v_ref, q_ref, y_ref), (ks, vs, qs, ys))):
            if shift == 0:
                block = src.at[:, own]
            elif half:
                block = received[i // 2][shift - 1].at[i % 2]
            else:
                block = received[0][shift - 1].at[i]
            copies.append(pltpu.make_async_copy(block, dst.at[rows], sem.at[shift, i]))
    run_copies(copies)

    block = 512

    def one_head(head, carry):
        cs = pl.ds(pl.multiple_of(head * DH, DH), DH)
        rest = 1.0 - g_ref[2 * half + head]
        for i in range(SEG // block):
            rows = slice(i * block, (i + 1) * block)
            last = (i + 1) * block
            old = last - block
            q, y = qs[rows, cs], ys[rows, cs]
            k, v = ks[:last, cs], vs[:last, cs]
            scores = dot(q, k, 1, 1)
            below = lax.broadcasted_iota(jnp.int32, (block, block), 0) >= lax.broadcasted_iota(
                jnp.int32, (block, block), 1
            )
            diagonal = jnp.where(below, scores[:, old:], -jnp.inf)
            scores = jnp.concatenate([scores[:, :old], diagonal], 1) if i else diagonal
            top = jnp.max(scores, 1, keepdims=True)
            powers = jnp.exp2((scores - top) * (SCALE * LOG2E))
            prob = powers * (1.0 / jnp.sum(powers, 1, keepdims=True))
            low = prob.astype(bf16)
            dprob = dot(y, v, 1, 1) * rest
            mean = jnp.sum(prob * dprob, 1, keepdims=True)
            dlow = (prob * (dprob - mean)).astype(bf16)
            local_ref[rows, cs] = dot(low, v, 1, 0)
            dq_ref[rows, cs] = dot(dlow, k, 1, 0) * SCALE
            dv, dk = dot(y, low, 0, 0), dot(q, dlow, 0, 0)
            if i:
                dvs[:, :old] += dv[:, :old]
                dks[:, :old] += dk[:, :old]
            dvs[:, old:last] = dv[:, old:]
            dks[:, old:last] = dk[:, old:]
        dkv_ref[0, :, cs] = (dks[...].T * SCALE).astype(bf16)
        dkv_ref[1, :, cs] = (dvs[...].T * rest).astype(bf16)
        if half:
            gate = g_ref[2 * half + head]
            memory = memory_of(mem_ref, 2 * half + head)
            for i in range(4):
                rows = slice(i * SHARE, (i + 1) * SHARE)
                q, y = qs[rows, cs].astype(f32), ys[rows, cs]
                _, _, retrieved, denom_grad, weight = read_rows(memory, gate, q, y)
                out, dq = results_of_rows(
                    memory, gate, q, y, retrieved, denom_grad, weight,
                    local_ref[rows, cs], dq_ref[rows, cs],
                )
                dkv_ref[2, rows, cs] = out
                dkv_ref[3, rows, cs] = dq
        return carry

    lax.fori_loop(0, 2, one_head, 0)
    if half:
        run_copies(
            [
                pltpu.make_async_copy(
                    dkv_ref.at[:, pl.ds(pl.multiple_of(group_of(z, i) * SHARE, SHARE), SHARE)],
                    out,
                    sem_out.at[i],
                )
                for i, out in enumerate(outs)
            ]
        )


def attention(z, gates, arrays, received, half, memory=()):
    seg_half = (SEG, HALF)
    last = [
        pltpu.SemaphoreType.DMA((4,)),
        pltpu.VMEM((4, SEG, HALF), bf16),
        pltpu.VMEM(seg_half, f32),
        pltpu.VMEM(seg_half, f32),
    ]
    return pl.pallas_call(
        functools.partial(attention_kernel, half=half),
        out_shape=[shape((4, SHARE, HALF))] * 4
        if half
        else [shape(seg_half, f32)] * 2 + [shape((2, SEG, HALF))],
        in_specs=[SMEM, SMEM] + [HBM] * (4 + 3 * (1 + half)) + [VMEM] * half,
        out_specs=[HBM] * 4 if half else [VMEM] * 3,
        scratch_shapes=[pltpu.VMEM(seg_half, bf16)] * 4
        + [pltpu.VMEM((DH, SEG), f32)] * 2
        + [pltpu.SemaphoreType.DMA((4, 4))]
        + last * half,
        compiler_params=params(60),
        cost_estimate=cost(12 if half else 10),
    )(z, gates, *arrays, *received, *memory)


def memory_kernel(
    z_ref, g_ref, mem_ref, q_ref, y_ref, a1, a2, a3, b1, b2, b3, local_ref, dq_ref, dkv_ref,
    mg_ref, o0, o1, o2, o3,
    qs, ys, ls, ds, kvs, sem, sem_f
):
    z = z_ref[0]
    own = pl.ds(pl.multiple_of(z * GROUP, GROUP), GROUP)
    copies = []
    for shift in range(4):
        for i, (src, dst) in enumerate(((q_ref, qs), (y_ref, ys))):
            if shift == 0:
                copies.append(
                    pltpu.make_async_copy(src.at[:, own], dst.at[0], sem.at[0, i, 0])
                )
                continue
            for half, block in enumerate(
                ((a1, a2, a3)[shift - 1].at[2 + i], (b1, b2, b3)[shift - 1].at[i])
            ):
                cols = pl.ds(half * HALF, HALF)
                copies.append(
                    pltpu.make_async_copy(block, dst.at[shift, :, cols], sem.at[shift, i, half])
                )
        rows = pl.ds(pl.multiple_of(group_of(z, -shift) * SHARE, SHARE), SHARE)
        for i, (src, dst) in enumerate(
            ((local_ref.at[rows], ls), (dq_ref.at[rows], ds), (dkv_ref.at[:, rows], kvs))
        ):
            copies.append(pltpu.make_async_copy(src, dst.at[shift], sem_f.at[shift, i]))
    run_copies(copies)
    outs = (o0, o3, o2, o1)
    for shift in range(4):
        outs[shift][:2] = kvs[shift]

    def one_head(head, carry, results):
        cs = pl.ds(pl.multiple_of(head * DH, DH), DH)
        gate = g_ref[head]
        memory = memory_of(mem_ref, head)
        grad = jnp.zeros((DH, 2 * DH), f32)
        norm_grad = jnp.zeros((1, DH), f32)
        for shift in range(4):
            q, y = qs[shift, :, cs].astype(f32), ys[shift, :, cs]
            phi_low, phi, retrieved, denom_grad, weight = read_rows(memory, gate, q, y)
            scaled = split(y.astype(f32) * weight)
            grad += dot(phi_low, jnp.concatenate(scaled, 1), 0, 0)
            norm_grad += jnp.sum(phi * denom_grad, 0, keepdims=True)
            if results:
                out, dq = results_of_rows(
                    memory, gate, q, y, retrieved, denom_grad, weight,
                    ls[shift, :, cs], ds[shift, :, cs],
                )
                outs[shift][2, :, cs] = out
                outs[shift][3, :, cs] = dq
        total = grad[:, :DH] + grad[:, DH:]
        at = pl.multiple_of(head * 8, 8)
        mg_ref[pl.ds(at, 8), :16, :] = total.reshape(8, 16, DH).astype(bf16)
        mg_ref[at, 16:32, :] = jnp.broadcast_to(norm_grad, (16, DH)).astype(bf16)
        return carry

    lax.fori_loop(0, 2, functools.partial(one_head, results=True), 0)
    lax.fori_loop(2, 4, functools.partial(one_head, results=False), 0)


def read_memory(z, gates, memory, q, y, in_a, qy_b, local):
    out = pl.pallas_call(
        memory_kernel,
        out_shape=[shape((32, 32, DH))] + [shape((4, SHARE, HALF))] * 4,
        in_specs=[SMEM, SMEM, VMEM] + [HBM] * 11,
        out_specs=[VMEM] * 5,
        scratch_shapes=[pltpu.VMEM((4, SHARE, GROUP), bf16)] * 2
        + [pltpu.VMEM((4, SHARE, HALF), f32)] * 2
        + [
            pltpu.VMEM((4, 2, SHARE, HALF), bf16),
            pltpu.SemaphoreType.DMA((4, 2, 2)),
            pltpu.SemaphoreType.DMA((4, 3)),
        ],
        compiler_params=params(60),
        cost_estimate=cost(8),
        name="read_memory",
    )(z, gates, memory, q, y, *in_a, *qy_b, *local)
    return out[0], out[1:]


def token_kernel(z_ref, *rest):
    firsts, seconds, (a_ref, b_ref) = rest[:4], rest[4:8], rest[8:]
    for shift in range(4):
        base = group_of(z_ref[0], -shift) * GROUP
        for half, pieces in enumerate((firsts, seconds)):
            cols = pl.ds(pl.multiple_of(base + half * HALF, HALF), HALF)
            a_ref[:, cols] = pieces[shift][0]
            b_ref[:, cols] = pieces[shift][1]


def results_of_tokens(z, firsts, seconds):
    piece = pl.BlockSpec((2, SHARE, HALF), lambda i: (1, 0, 0))
    whole = pl.BlockSpec((SHARE, 4 * GROUP), lambda i: (0, 0))
    return pl.pallas_call(
        token_kernel,
        grid=(1,),
        out_shape=[shape((SHARE, 4 * GROUP))] * 2,
        in_specs=[SMEM] + [piece] * 8,
        out_specs=[whole] * 2,
        compiler_params=params(16),
        cost_estimate=cost(3),
        name="results",
    )(z, *firsts, *seconds)


def compact_kernel(in_ref, out_ref):
    out_ref[:GROUP] = in_ref[:, :16, :].reshape(GROUP, DH)
    for head in range(HEADS):
        out_ref[GROUP + 16 * head : GROUP + 16 * head + 16] = in_ref[8 * head, 16:32, :]


def compact(x):
    return pl.pallas_call(
        compact_kernel,
        out_shape=shape((ROWS, DH)),
        in_specs=[VMEM],
        out_specs=VMEM,
        compiler_params=params(8),
        cost_estimate=cost(2),
        name="compact",
    )(x)


def key_value_kernel(z_ref, k_ref, v_ref, *rest):
    backs, firsts, seconds = rest[:4], rest[4:8], rest[8:12]
    kg_ref, vg_ref = rest[12:]
    for shift in range(4):

        @pl.when(pl.program_id(0) == shift)
        def _():
            for head in range(HEADS):
                cols = slice(head * DH, (head + 1) * DH)
                inner = slice((head % 2) * DH, (head % 2 + 1) * DH)
                grads = (firsts, seconds)[head // 2][shift]
                back = backs[shift][cols]
                norm = backs[shift][GROUP + 16 * head : GROUP + 16 * head + 16].astype(f32)[:1]
                k = k_ref[:, cols].astype(f32)
                v = v_ref[:, cols]
                kg = grads[0, :, inner].astype(f32) + (dot(v, back, 1, 1) + norm) * slope(k)
                kg_ref[:, cols] = kg.astype(bf16)
                vg = grads[1, :, inner].astype(f32) + dot(feature(k).astype(bf16), back, 1, 0)
                vg_ref[:, cols] = vg.astype(bf16)


def key_value(z, keys, values, backs, firsts, seconds):
    piece = pl.BlockSpec((2, SHARE, HALF), lambda i, z: (0, 0, 0))
    group = pl.BlockSpec((SHARE, GROUP), lambda i, z: (0, lax.rem(z[0] + 4 - i, 4)))
    state = pl.BlockSpec((ROWS, DH), lambda i, z: (0, 0))
    return pl.pallas_call(
        key_value_kernel,
        grid_spec=pltpu.PrefetchScalarGridSpec(
            num_scalar_prefetch=1,
            grid=(4,),
            in_specs=[group] * 2 + [state] * 4 + [piece] * 8,
            out_specs=[group] * 2,
        ),
        out_shape=[shape((SHARE, 4 * GROUP))] * 2,
        compiler_params=params(24),
        cost_estimate=cost(5),
        name="key_value",
    )(z, keys, values, *backs, *firsts, *seconds)


def to_peers(blocks):
    sent = []
    for shift, block in enumerate(blocks, 1):
        sent.append(lax.ppermute(block, "head", [(i, (i + shift) % 4) for i in range(4)]))
    return sent


def swap(x):
    return lax.all_to_all(x, "seq", 0, 0, tiled=True)


def body(k, v, q, y, gate_logits):
    z = lax.axis_index("head").astype(jnp.int32).reshape(1)
    gates = jax.nn.sigmoid(gate_logits)
    arrays = (k, v, q, y)
    partials, own, first, queries_b, keys_b = front(z, *arrays)
    partials = to_peers(partials)
    in_a = to_peers(first)
    qy_b = to_peers(queries_b)
    kv_b = to_peers(keys_b)
    slices = swap(update(own, partials))
    memory = swap(scan(slices, False))
    local = attention(z, gates, arrays, in_a, 0)
    grads, out_a = read_memory(z, gates, memory, q, y, in_a, qy_b, local)
    back_a = to_peers(out_a[1:])
    slices = swap(grads)
    out_b = attention(z, gates, arrays, kv_b + qy_b, 1, [memory])
    back_b = to_peers(out_b[1:])
    state = compact(swap(scan(slices, True)))
    states = [state] + to_peers([state] * 3)
    firsts, seconds = [out_a[0], *back_a], [out_b[0], *back_b]
    output, query_grad = results_of_tokens(z, firsts, seconds)
    key_grad, value_grad = key_value(z, k, v, states, firsts, seconds)
    return output, query_grad, key_grad, value_grad


def whole(queries, key_rows, values, gate_logits, out_grad):
    return body(key_rows, values, queries, out_grad, gate_logits)


def solution(mesh):
    spec = P(("seq", "head"), None)
    return jax.shard_map(
        whole,
        mesh=mesh,
        in_specs=(spec, spec, spec, P("head"), spec),
        out_specs=(spec,) * 4,
        check_vma=False,
    )
```

```python
import functools

import jax
import jax.numpy as jnp
from jax import lax
from jax.experimental import pallas as pl
from jax.experimental.pallas import tpu as pltpu
from jax.sharding import PartitionSpec as P


DH = 128
HEADS = 4
HALF = 2 * DH
GROUP = HEADS * DH
ROWS = GROUP + 16 * HEADS
SHARE = 256
SEG = 4 * SHARE
SCALE = DH ** (-0.5)
LOG2E = 1.4426950408889634
f32 = jnp.float32
bf16 = jnp.bfloat16

HBM = pl.BlockSpec(memory_space=pltpu.HBM)
VMEM = pl.BlockSpec(memory_space=pltpu.VMEM)
SMEM = pl.BlockSpec(memory_space=pltpu.SMEM)


def shape(dims, dtype=bf16):
    return jax.ShapeDtypeStruct(dims, dtype)


def params(mib=56):
    return pltpu.CompilerParams(vmem_limit_bytes=mib << 20)


def cost(us):
    return pl.CostEstimate(flops=int(us * 5e8), bytes_accessed=int(us * 2e6), transcendentals=0)


def dot(a, b, ca, cb):
    return lax.dot_general(a, b, (((ca,), (cb,)), ((), ())), preferred_element_type=f32)


def feature(x):
    return jnp.where(x > 0, x + 1.0, jnp.exp(jnp.minimum(x, 0.0)))


def slope(x):
    return jnp.where(x > 0, jnp.ones_like(x), jnp.exp(jnp.minimum(x, 0.0)))


def split(x):
    high = x.astype(bf16)
    return high, (x - high.astype(f32)).astype(bf16)


def group_of(z, shift):
    return lax.rem(z + shift + 4, 4)


def partial_kernel(z_ref, k_ref, v_ref, *outs):
    for step in range(4):

        @pl.when(pl.program_id(0) == step)
        def _():
            out = outs[step]
            for head in range(HEADS):
                cols = slice(head * DH, (head + 1) * DH)
                phi = feature(k_ref[:, cols].astype(f32)).astype(bf16)
                out[cols] = dot(phi, v_ref[:, cols], 0, 0).astype(out.dtype)
                sums = jnp.sum(phi.astype(f32), axis=0, keepdims=True)
                high = sums.astype(bf16).astype(f32)
                first = lax.broadcasted_iota(jnp.int32, (16, DH), 0) == 0
                rows = jnp.where(first, jnp.broadcast_to(high, (16, DH)), sums - high)
                out[GROUP + 16 * head : GROUP + 16 * head + 16] = rows.astype(out.dtype)


def partial_updates(z, k, v):
    group = pl.BlockSpec((SHARE, GROUP), lambda i, z: (0, lax.rem(z[0] + 1 + i, 4)))
    state = pl.BlockSpec((ROWS, DH), lambda i, z: (0, 0))
    out = pl.pallas_call(
        partial_kernel,
        grid_spec=pltpu.PrefetchScalarGridSpec(
            num_scalar_prefetch=1, grid=(4,), in_specs=[group] * 2, out_specs=[state] * 4
        ),
        out_shape=[shape((ROWS, DH))] * 3 + [shape((ROWS, DH), f32)],
        compiler_params=params(60),
        cost_estimate=cost(3),
        name="partial",
    )(z, k, v)
    return out[:3], out[3]


def pack_kernel(z_ref, k_ref, v_ref, q_ref, y_ref, *rest):
    outs = (rest[:3], rest[3:6], rest[6:9])
    buf, sem_in, sem_out = rest[9:]
    z = z_ref[0]
    loads, stores = [], []
    for shift in (1, 2, 3):
        at = pl.multiple_of(group_of(z, shift) * GROUP, GROUP)
        for i, src in enumerate((k_ref, v_ref, q_ref, y_ref)):
            copy = pltpu.make_async_copy(
                src.at[:, pl.ds(at, GROUP)], buf.at[shift - 1, i], sem_in.at[shift - 1, i]
            )
            copy.start()
            loads.append(copy)
    for shift in (1, 2, 3):
        first, queries, keys = [group[shift - 1] for group in outs]
        for i in range(4):
            loads[4 * (shift - 1) + i].wait()
            part, sem = buf.at[shift - 1, i], sem_out.at[shift - 1, i]
            second = keys.at[i] if i < 2 else queries.at[i - 2]
            for half, out in enumerate((first.at[i], second)):
                copy = pltpu.make_async_copy(
                    part.at[:, pl.ds(half * HALF, HALF)], out, sem.at[half]
                )
                copy.start()
                stores.append(copy)
    for copy in stores:
        copy.wait()


def pack(z, k, v, q, y):
    out = pl.pallas_call(
        pack_kernel,
        out_shape=[shape((4, SHARE, HALF))] * 3 + [shape((2, SHARE, HALF))] * 6,
        in_specs=[SMEM] + [HBM] * 4,
        out_specs=[HBM] * 9,
        scratch_shapes=[
            pltpu.VMEM((3, 4, SHARE, GROUP), bf16),
            pltpu.SemaphoreType.DMA((3, 4)),
            pltpu.SemaphoreType.DMA((3, 4, 2)),
        ],
        compiler_params=params(60),
        cost_estimate=cost(4),
        name="pack",
    )(z, k, v, q, y)
    return out[:3], out[3:6], out[6:9]


def update_kernel(own, r1, r2, r3, out_ref):
    for head in range(HEADS):
        rows = slice(head * DH, (head + 1) * DH)
        total = own[rows]
        for piece in (r1, r2, r3):
            total += piece[rows].astype(f32)
        out_ref[8 * head : 8 * head + 8, :16, :] = total.reshape(8, 16, DH)
        rows = slice(GROUP + 16 * head, GROUP + 16 * head + 16)
        sums = own[rows]
        for piece in (r1, r2, r3):
            sums += piece[rows].astype(f32)
        out_ref[8 * head, 16:24, :] = jnp.broadcast_to(sums[:1] + sums[1:2], (8, DH))


def update(own, received):
    return pl.pallas_call(
        update_kernel,
        out_shape=shape((32, 24, DH), f32),
        in_specs=[VMEM] * 4,
        out_specs=VMEM,
        compiler_params=params(8),
        cost_estimate=cost(2),
        name="update",
    )(own, *received)


def scan_kernel(in_ref, out_ref, buf, res, sem_in, sem_out, *, reverse):
    count, parts = in_ref.shape[0], 4
    each = count // parts
    order = list(range(parts))[::-1] if reverse else list(range(parts))
    loads, stores = [], []
    for part in range(parts):
        at = pl.ds(part * each, each)
        loads.append(pltpu.make_async_copy(in_ref.at[at], buf.at[at], sem_in.at[part]))
        stores.append(pltpu.make_async_copy(res.at[at], out_ref.at[at], sem_out.at[part]))
    for part in order:
        loads[part].start()
    total = jnp.zeros(in_ref.shape[1:], f32)
    for part in order:
        loads[part].wait()
        for step in range(each):
            at = part * each + (each - 1 - step if reverse else step)
            res[at] = total.astype(res.dtype)
            total += buf[at].astype(f32)
        stores[part].start()
    for copy in stores:
        copy.wait()


def scan(x, reverse):
    return pl.pallas_call(
        functools.partial(scan_kernel, reverse=reverse),
        out_shape=shape(x.shape, x.dtype),
        in_specs=[HBM],
        out_specs=HBM,
        scratch_shapes=[pltpu.VMEM(x.shape, x.dtype)] * 2 + [pltpu.SemaphoreType.DMA((4,))] * 2,
        compiler_params=params(12),
        cost_estimate=cost(2),
        name="scan_later" if reverse else "scan_earlier",
    )(x)


def memory_of(mem_ref, head):
    at = pl.multiple_of(head * 8, 8)
    memory = mem_ref[pl.ds(at, 8), :16, :].reshape(DH, DH)
    high, low = split(memory)
    norm = mem_ref[at, 16:24, :][:1]
    return jnp.concatenate([high, low], 1), jnp.concatenate([high, low], 0), norm


def read_rows(memory, gate, q, y_low):
    right, _, norm = memory
    y = y_low.astype(f32)
    phi_low = feature(q).astype(bf16)
    phi = phi_low.astype(f32)
    both = dot(phi_low, right, 1, 0)
    raw = jnp.sum(phi * norm, 1, keepdims=True)
    inverse = 1.0 / jnp.maximum(raw, 1.0)
    retrieved = (both[:, :DH] + both[:, DH:]) * inverse
    denom_grad = jnp.where(
        raw > 1.0, -gate * jnp.sum(y * retrieved, 1, keepdims=True) * inverse, 0.0
    )
    return phi_low, phi, retrieved, denom_grad, gate * inverse


def results_of_rows(memory, gate, q, y_low, retrieved, denom_grad, weight, local, dq):
    _, below, norm = memory
    both = dot(y_low, below, 1, 1)
    back = (both[:, :DH] + both[:, DH:]) * weight + denom_grad * norm
    out = gate * retrieved + (1.0 - gate) * local
    return out.astype(bf16), (dq + back * slope(q)).astype(bf16)


def attention_kernel(
    z_ref, g_ref, k_ref, v_ref, q_ref, y_ref, *refs, half
):
    refs = list(refs)
    received = [[refs.pop(0) for _ in range(3)] for _ in range(1 + half)]
    mem_ref = refs.pop(0) if half else None
    outs = [refs.pop(0) for _ in range(4 if half else 3)]
    local_ref, dq_ref, dkv_ref, sem_out = [refs.pop() for _ in range(4)]
    ks, vs, qs, ys, dks, dvs, sem = refs
    z = z_ref[0]
    loads, stores = ([], []), []
    for head in range(2):
        cs = pl.ds(head * DH, DH)
        own = pl.ds(pl.multiple_of(z * GROUP + half * HALF + head * DH, DH), DH)
        for shift in range(4):
            rows = pl.ds(pl.multiple_of(group_of(z, -shift) * SHARE, SHARE), SHARE)
            for i, (src, dst) in enumerate(zip((k_ref, v_ref, q_ref, y_ref), (ks, vs, qs, ys))):
                if shift == 0:
                    block = src.at[:, own]
                elif half:
                    block = received[i // 2][shift - 1].at[i % 2, :, cs]
                else:
                    block = received[0][shift - 1].at[i, :, cs]
                copy = pltpu.make_async_copy(block, dst.at[rows, cs], sem.at[head, shift, i])
                copy.start()
                loads[head].append(copy)

    block = 512

    for head in range(2):
        cs = slice(head * DH, (head + 1) * DH)
        for copy in loads[head]:
            copy.wait()
        rest = 1.0 - g_ref[2 * half + head]
        for i in range(SEG // block):
            rows = slice(i * block, (i + 1) * block)
            last = (i + 1) * block
            old = last - block
            q, y = qs[rows, cs], ys[rows, cs]
            k, v = ks[:last, cs], vs[:last, cs]
            scores = dot(q, k, 1, 1)
            below = lax.broadcasted_iota(jnp.int32, (block, block), 0) >= lax.broadcasted_iota(
                jnp.int32, (block, block), 1
            )
            diagonal = jnp.where(below, scores[:, old:], -jnp.inf)
            scores = jnp.concatenate([scores[:, :old], diagonal], 1) if i else diagonal
            top = jnp.max(scores, 1, keepdims=True)
            powers = jnp.exp2((scores - top) * (SCALE * LOG2E))
            prob = powers * (1.0 / jnp.sum(powers, 1, keepdims=True))
            low = prob.astype(bf16)
            dprob = dot(y, v, 1, 1) * rest
            mean = jnp.sum(prob * dprob, 1, keepdims=True)
            dlow = (prob * (dprob - mean)).astype(bf16)
            local_ref[rows, cs] = dot(low, v, 1, 0)
            dq_ref[rows, cs] = dot(dlow, k, 1, 0) * SCALE
            dv, dk = dot(y, low, 0, 0), dot(q, dlow, 0, 0)
            if i:
                dvs[:, :old] += dv[:, :old]
                dks[:, :old] += dk[:, :old]
            dvs[:, old:last] = dv[:, old:]
            dks[:, old:last] = dk[:, old:]
        dkv_ref[0, :, cs] = (dks[...].T * SCALE).astype(bf16)
        dkv_ref[1, :, cs] = (dvs[...].T * rest).astype(bf16)
        if half:
            gate = g_ref[2 * half + head]
            memory = memory_of(mem_ref, 2 * half + head)
            for i in range(4):
                rows = slice(i * SHARE, (i + 1) * SHARE)
                q, y = qs[rows, cs].astype(f32), ys[rows, cs]
                _, _, retrieved, denom_grad, weight = read_rows(memory, gate, q, y)
                out, dq = results_of_rows(
                    memory, gate, q, y, retrieved, denom_grad, weight,
                    local_ref[rows, cs], dq_ref[rows, cs],
                )
                dkv_ref[2, rows, cs] = out
                dkv_ref[3, rows, cs] = dq
        if half:
            pairs = []
            for i, out in enumerate(outs):
                rows = pl.ds(pl.multiple_of(group_of(z, i) * SHARE, SHARE), SHARE)
                pairs.append((dkv_ref.at[:, rows, cs], out.at[:, :, cs]))
        else:
            pairs = [
                (local_ref.at[:, cs], outs[0].at[:, cs]),
                (dq_ref.at[:, cs], outs[1].at[:, cs]),
                (dkv_ref.at[:, :, cs], outs[2].at[:, :, cs]),
            ]
        for i, (src, dst) in enumerate(pairs):
            copy = pltpu.make_async_copy(src, dst, sem_out.at[head, i])
            copy.start()
            stores.append(copy)
    for copy in stores:
        copy.wait()


def attention(z, gates, arrays, received, half, memory=()):
    seg_half = (SEG, HALF)
    last = [
        pltpu.SemaphoreType.DMA((2, 4)),
        pltpu.VMEM((4 if half else 2, SEG, HALF), bf16),
        pltpu.VMEM(seg_half, f32),
        pltpu.VMEM(seg_half, f32),
    ]
    return pl.pallas_call(
        functools.partial(attention_kernel, half=half),
        out_shape=[shape((4, SHARE, HALF))] * 4
        if half
        else [shape(seg_half, f32)] * 2 + [shape((2, SEG, HALF))],
        in_specs=[SMEM, SMEM] + [HBM] * (4 + 3 * (1 + half)) + [VMEM] * half,
        out_specs=[HBM] * (4 if half else 3),
        scratch_shapes=[pltpu.VMEM(seg_half, bf16)] * 4
        + [pltpu.VMEM((DH, SEG), f32)] * 2
        + [pltpu.SemaphoreType.DMA((2, 4, 4))]
        + last,
        compiler_params=params(60),
        cost_estimate=cost(12 if half else 10),
    )(z, gates, *arrays, *received, *memory)


def memory_kernel(
    z_ref, g_ref, mem_ref, q_ref, y_ref, a1, a2, a3, b1, b2, b3, local_ref, dq_ref, dkv_ref,
    mg_ref, o0, o1, o2, o3,
    qs, ys, ls, ds, kvs, sem, sem_f
):
    z = z_ref[0]
    copies = ([], [])
    for half in (1, 0):
        cols = pl.ds(half * HALF, HALF)
        own = pl.ds(pl.multiple_of(z * GROUP + half * HALF, HALF), HALF)
        for shift in range(4):
            for i, (src, dst) in enumerate(((q_ref, qs), (y_ref, ys))):
                if shift == 0:
                    block = src.at[:, own]
                elif half:
                    block = (b1, b2, b3)[shift - 1].at[i]
                else:
                    block = (a1, a2, a3)[shift - 1].at[2 + i]
                copies[half].append(
                    pltpu.make_async_copy(block, dst.at[shift, :, cols], sem.at[shift, i, half])
                )
    for shift in range(4):
        rows = pl.ds(pl.multiple_of(group_of(z, -shift) * SHARE, SHARE), SHARE)
        for i, (src, dst) in enumerate(
            ((local_ref.at[rows], ls), (dq_ref.at[rows], ds), (dkv_ref.at[:, rows], kvs))
        ):
            copies[0].append(pltpu.make_async_copy(src, dst.at[shift], sem_f.at[shift, i]))
    for copy in copies[1] + copies[0]:
        copy.start()
    outs = (o0, o3, o2, o1)

    def one_head(head, carry, results):
        cs = pl.ds(pl.multiple_of(head * DH, DH), DH)
        gate = g_ref[head]
        memory = memory_of(mem_ref, head)
        grad = jnp.zeros((DH, 2 * DH), f32)
        norm_grad = jnp.zeros((1, DH), f32)
        for shift in range(4):
            q, y = qs[shift, :, cs].astype(f32), ys[shift, :, cs]
            phi_low, phi, retrieved, denom_grad, weight = read_rows(memory, gate, q, y)
            scaled = split(y.astype(f32) * weight)
            grad += dot(phi_low, jnp.concatenate(scaled, 1), 0, 0)
            norm_grad += jnp.sum(phi * denom_grad, 0, keepdims=True)
            if results:
                out, dq = results_of_rows(
                    memory, gate, q, y, retrieved, denom_grad, weight,
                    ls[shift, :, cs], ds[shift, :, cs],
                )
                outs[shift][2, :, cs] = out
                outs[shift][3, :, cs] = dq
        total = grad[:, :DH] + grad[:, DH:]
        at = pl.multiple_of(head * 8, 8)
        mg_ref[pl.ds(at, 8), :16, :] = total.reshape(8, 16, DH).astype(bf16)
        mg_ref[at, 16:32, :] = jnp.broadcast_to(norm_grad, (16, DH)).astype(bf16)
        return carry

    for copy in copies[1]:
        copy.wait()
    lax.fori_loop(2, 4, functools.partial(one_head, results=False), 0)
    for copy in copies[0]:
        copy.wait()
    for shift in range(4):
        outs[shift][:2] = kvs[shift]
    lax.fori_loop(0, 2, functools.partial(one_head, results=True), 0)


def read_memory(z, gates, memory, q, y, in_a, qy_b, local):
    out = pl.pallas_call(
        memory_kernel,
        out_shape=[shape((32, 32, DH))] + [shape((4, SHARE, HALF))] * 4,
        in_specs=[SMEM, SMEM, VMEM] + [HBM] * 11,
        out_specs=[VMEM] * 5,
        scratch_shapes=[pltpu.VMEM((4, SHARE, GROUP), bf16)] * 2
        + [pltpu.VMEM((4, SHARE, HALF), f32)] * 2
        + [
            pltpu.VMEM((4, 2, SHARE, HALF), bf16),
            pltpu.SemaphoreType.DMA((4, 2, 2)),
            pltpu.SemaphoreType.DMA((4, 3)),
        ],
        compiler_params=params(60),
        cost_estimate=cost(8),
        name="read_memory",
    )(z, gates, memory, q, y, *in_a, *qy_b, *local)
    return out[0], out[1:]


def token_kernel(z_ref, *rest):
    firsts, seconds, (a_ref, b_ref) = rest[:4], rest[4:8], rest[8:]
    for shift in range(4):
        base = group_of(z_ref[0], -shift) * GROUP
        for half, pieces in enumerate((firsts, seconds)):
            cols = pl.ds(pl.multiple_of(base + half * HALF, HALF), HALF)
            a_ref[:, cols] = pieces[shift][0]
            b_ref[:, cols] = pieces[shift][1]


def results_of_tokens(z, firsts, seconds):
    piece = pl.BlockSpec((2, SHARE, HALF), lambda i: (1, 0, 0))
    whole = pl.BlockSpec((SHARE, 4 * GROUP), lambda i: (0, 0))
    return pl.pallas_call(
        token_kernel,
        grid=(1,),
        out_shape=[shape((SHARE, 4 * GROUP))] * 2,
        in_specs=[SMEM] + [piece] * 8,
        out_specs=[whole] * 2,
        compiler_params=params(16),
        cost_estimate=cost(3),
        name="results",
    )(z, *firsts, *seconds)


def compact_kernel(in_ref, out_ref):
    out_ref[:GROUP] = in_ref[:, :16, :].reshape(GROUP, DH)
    for head in range(HEADS):
        out_ref[GROUP + 16 * head : GROUP + 16 * head + 16] = in_ref[8 * head, 16:32, :]


def compact(x):
    return pl.pallas_call(
        compact_kernel,
        out_shape=shape((ROWS, DH)),
        in_specs=[VMEM],
        out_specs=VMEM,
        compiler_params=params(8),
        cost_estimate=cost(2),
        name="compact",
    )(x)


def key_value_kernel(z_ref, k_ref, v_ref, *rest):
    backs, firsts, seconds = rest[:4], rest[4:8], rest[8:12]
    kg_ref, vg_ref = rest[12:]
    for shift in range(4):

        @pl.when(pl.program_id(0) == shift)
        def _():
            for head in range(HEADS):
                cols = slice(head * DH, (head + 1) * DH)
                inner = slice((head % 2) * DH, (head % 2 + 1) * DH)
                grads = (firsts, seconds)[head // 2][shift]
                back = backs[shift][cols]
                norm = backs[shift][GROUP + 16 * head : GROUP + 16 * head + 16].astype(f32)[:1]
                k = k_ref[:, cols].astype(f32)
                v = v_ref[:, cols]
                kg = grads[0, :, inner].astype(f32) + (dot(v, back, 1, 1) + norm) * slope(k)
                kg_ref[:, cols] = kg.astype(bf16)
                vg = grads[1, :, inner].astype(f32) + dot(feature(k).astype(bf16), back, 1, 0)
                vg_ref[:, cols] = vg.astype(bf16)


def key_value(z, keys, values, backs, firsts, seconds):
    piece = pl.BlockSpec((2, SHARE, HALF), lambda i, z: (0, 0, 0))
    group = pl.BlockSpec((SHARE, GROUP), lambda i, z: (0, lax.rem(z[0] + 4 - i, 4)))
    state = pl.BlockSpec((ROWS, DH), lambda i, z: (0, 0))
    return pl.pallas_call(
        key_value_kernel,
        grid_spec=pltpu.PrefetchScalarGridSpec(
            num_scalar_prefetch=1,
            grid=(4,),
            in_specs=[group] * 2 + [state] * 4 + [piece] * 8,
            out_specs=[group] * 2,
        ),
        out_shape=[shape((SHARE, 4 * GROUP))] * 2,
        compiler_params=params(24),
        cost_estimate=cost(5),
        name="key_value",
    )(z, keys, values, *backs, *firsts, *seconds)


def to_peers(blocks):
    sent = []
    for shift, block in enumerate(blocks, 1):
        sent.append(lax.ppermute(block, "head", [(i, (i + shift) % 4) for i in range(4)]))
    return sent


def swap(x):
    return lax.all_to_all(x, "seq", 0, 0, tiled=True)


def body(k, v, q, y, gate_logits):
    z = lax.axis_index("head").astype(jnp.int32).reshape(1)
    gates = jax.nn.sigmoid(gate_logits)
    arrays = (k, v, q, y)
    partials, own = partial_updates(z, k, v)
    first, queries_b, keys_b = pack(z, k, v, q, y)
    partials = to_peers(partials)
    in_a = to_peers(first)
    qy_b = to_peers(queries_b)
    kv_b = to_peers(keys_b)
    slices = swap(update(own, partials))
    memory = swap(scan(slices, False))
    local = attention(z, gates, arrays, in_a, 0)
    grads, out_a = read_memory(z, gates, memory, q, y, in_a, qy_b, local)
    back_a = to_peers(out_a[1:])
    slices = swap(grads)
    out_b = attention(z, gates, arrays, kv_b + qy_b, 1, [memory])
    back_b = to_peers(out_b[1:])
    state = compact(swap(scan(slices, True)))
    states = [state] + to_peers([state] * 3)
    firsts, seconds = [out_a[0], *back_a], [out_b[0], *back_b]
    output, query_grad = results_of_tokens(z, firsts, seconds)
    key_grad, value_grad = key_value(z, k, v, states, firsts, seconds)
    return output, query_grad, key_grad, value_grad


def whole(queries, key_rows, values, gate_logits, out_grad):
    return body(key_rows, values, queries, out_grad, gate_logits)


def solution(mesh):
    spec = P(("seq", "head"), None)
    return jax.shard_map(
        whole,
        mesh=mesh,
        in_specs=(spec, spec, spec, P("head"), spec),
        out_specs=(spec,) * 4,
        check_vma=False,
    )
```
